128 devices in a mesh: ctx: 16 (over z_lo, x, core), tp: 8 (over y, z_hi).
Axes of the slice: x: 4, y: 4, z: 4 (z_hi: 2, z_lo: 2; z = z_hi * 2 + z_lo), core: 2. Of those that a mesh axis runs over, the one named last changes fastest.
Arguments:
- queries: bfloat16 [4096, 8192], P(('ctx', 'tp')), may hold values from -5.5 to 5.5
- keys: bfloat16 [4096, 1024], P(('ctx', 'tp')), may hold values from -5.5 to 5.5
- values: bfloat16 [4096, 1024], P(('ctx', 'tp')), may hold values from -6 to 6
- out_grad: bfloat16 [4096, 8192], P(('ctx', 'tp')), may hold values from -6 to 6
- doc_ids: int32 [4096], replicated, may hold values from 0 to 3, never falling along the last dimension, each value on 1 to 3840 neighbouring positions
Outputs:
- attended: float32 [4096, 8192], P(('ctx', 'tp'))
- query_grad: float32 [4096, 8192], P(('ctx', 'tp'))
- key_grad: float32 [4096, 1024], P(('ctx', 'tp'))
- value_grad: float32 [4096, 1024], P(('ctx', 'tp'))
The draws below stay inside these ranges and needn't reach their ends.
Inputs may be any that keep to these rules, and one draw needn't show every extreme that they name: doc_ids never falls along the sequence; each document holds 3840 tokens or fewer, and one holds exactly 3840.
All inputs are finite; a program needn't handle non-finite values.
Results may differ from the reference program's by a relative error of at most 0.019.
Values may be sent and summed in bfloat16 or wider, within the bound.
No kernel may reach another device: no remote copies, remote signals or barrier semaphores. Data moves between devices by JAX's collectives and lax.ppermute only.
A program may use at most 64 MiB of HBM per device.

```python
import math
import jax
import jax.numpy as jnp
import numpy as np
from jax import lax

HD = 128
GROUP = 8
KV = 8
HEADS = 64
TOK_CTX = 256
DOCS = 4
REACH = 15
TOKENS = 4096
MOST_DOC = 3840
N_CTX = 16


def paired_draw(key):
    base = jax.random.fold_in(key, 11)
    streams = jax.random.split(base, 2)
    query_all = jnp.clip(jax.random.normal(streams[0], (TOKENS, HEADS * HD), jnp.float32), -5.5, 5.5)
    key_all = jnp.clip(jax.random.normal(streams[1], (TOKENS, KV * HD), jnp.float32), -5.5, 5.5)
    return (query_all, key_all)


def draw_queries(key, part):
    return paired_draw(key)[0].astype(jnp.bfloat16)


def draw_keys(key, part):
    return paired_draw(key)[1].astype(jnp.bfloat16)


def levels(rng, shape, cuts, smallest, largest):
    factor_of = 1.0
    for position, parts in cuts:
        draws = jax.random.uniform(jax.random.fold_in(jax.random.fold_in(rng, 6), position), (parts,), jnp.float32, smallest / len(cuts), largest / len(cuts))
        factor_of = factor_of * jnp.repeat(jnp.exp(draws), shape[position] // parts).reshape((-1,) + (1,) * (len(shape) - 1 - position))
    return factor_of


def split_up(count, total, bound, lean):
    loads = [(1 << 20) // math.isqrt(grade ** lean) + 1 for grade in range(2, count + 1)]
    spare, holding = total - bound - (count - 1), [1] * (count - 1)
    while spare > 0:
        movable = [i for i in range(count - 1) if holding[i] < bound]
        pool, remaining = sum([loads[i] for i in movable]), spare
        for i in movable:
            more = min(bound - holding[i], max(1, remaining * loads[i] // pool), spare)
            holding[i] = holding[i] + more
            spare = spare - more
    return np.array([bound] + holding)


def uneven_parts(own_key, count, total, reach, slope):
    if count == 2:
        one = jax.random.randint(own_key, (), max(1, total - reach), min(reach, total - 1) + 1)
        return jnp.stack([one, total - one])
    sizes = jnp.asarray(split_up(count, total, reach, slope), jnp.int32)
    couples = (count - 1) // 2
    giver, receiver = sizes[1:1 + 2 * couples:2], sizes[2:2 + 2 * couples:2]
    room = jnp.minimum(giver - 1, reach - receiver)
    moved = jax.random.randint(jax.random.fold_in(own_key, 1), (couples,), 0, 1 << 20) % (room + 1)
    sizes = sizes.at[1:1 + 2 * couples:2].set(giver - moved).at[2:2 + 2 * couples:2].set(receiver + moved)
    return sizes[jax.random.permutation(jax.random.fold_in(own_key, 2), count)]


def noise(own_key, dims, scale, limit, cuts=(), kind=jnp.bfloat16):
    loudness = levels(own_key, dims, cuts, -0.22, 0.18) if cuts else 1.0
    drawn = jax.random.normal(own_key, dims, jnp.float32) * scale * loudness
    return jnp.minimum(jnp.maximum(drawn, -limit), limit).astype(kind)


def setup_inputs(seed: int = 0) -> dict:
    key_list = jax.random.split(jax.random.key(seed), 6)
    return {
        "queries": draw_queries(jax.random.fold_in(key_list[5], 71), 0),
        "keys": draw_keys(jax.random.fold_in(key_list[5], 71), 0),
        "values": noise(key_list[2], (TOKENS, KV * HD), 1.0, 6.0, ((0, 128),)),
        "out_grad": noise(key_list[3], (TOKENS, HEADS * HD), 1.0, 6.0, ((0, 128),)),
        "doc_ids": jnp.searchsorted(jnp.cumsum(uneven_parts(key_list[4], DOCS, TOKENS, MOST_DOC, 2)), jnp.arange(TOKENS), side="right").astype(jnp.int32),
    }


very_low = -1e30


def reference(queries, keys, values, out_grad, doc_ids):
    width = REACH * TOK_CTX
    span = width + TOK_CTX
    score_scale = HD ** -0.5
    highest = lax.Precision.HIGHEST
    query_heads = queries.reshape(TOKENS, KV, GROUP, HD).transpose(1, 0, 2, 3)
    grad_heads = out_grad.reshape(TOKENS, KV, GROUP, HD).transpose(1, 0, 2, 3)
    key_heads = keys.reshape(TOKENS, KV, HD).transpose(1, 0, 2)
    value_heads = values.reshape(TOKENS, KV, HD).transpose(1, 0, 2)
    doc_whole = doc_ids.astype(jnp.int32)
    doc_padded = jnp.concatenate([jnp.full((width,), -1, jnp.int32), doc_whole])

    def one_group(operands):
        query_one, key_one, value_one, grad_one = operands
        key_padded = jnp.concatenate([jnp.zeros((width, HD), key_one.dtype), key_one], 0)
        value_padded = jnp.concatenate([jnp.zeros((width, HD), value_one.dtype), value_one], 0)

        def advance(carry, shard):
            key_accum, value_accum = carry
            first = (shard * TOK_CTX).astype(jnp.int32)
            query_block = lax.dynamic_slice_in_dim(query_one, first, TOK_CTX, 0).astype(jnp.float32)
            grad_block = lax.dynamic_slice_in_dim(grad_one, first, TOK_CTX, 0).astype(jnp.float32)
            key_window = lax.dynamic_slice_in_dim(key_padded, first, span, 0).astype(jnp.float32)
            value_window = lax.dynamic_slice_in_dim(value_padded, first, span, 0).astype(jnp.float32)
            query_pos = first + jnp.arange(TOK_CTX, dtype=jnp.int32)
            key_pos = first - width + jnp.arange(span, dtype=jnp.int32)
            query_doc = lax.dynamic_slice_in_dim(doc_whole, first, TOK_CTX, 0)
            key_doc = lax.dynamic_slice_in_dim(doc_padded, first, span, 0)
            allowed = (key_pos[None, :] <= query_pos[:, None]) & (key_doc[None, :] == query_doc[:, None])
            scores = jnp.einsum("ihd,jd->hij", query_block, key_window, precision=highest) * score_scale
            scores = jnp.where(allowed[None], scores, very_low)
            top = jnp.max(scores, axis=-1, keepdims=True)
            total = jnp.sum(jnp.where(allowed[None], jnp.exp(scores - top), 0.0), axis=-1, keepdims=True)
            log_total = top + jnp.log(total)
            attn_prob = jnp.where(allowed[None], jnp.exp(scores - log_total), 0.0)
            prob_half = lax.optimization_barrier(attn_prob.astype(jnp.bfloat16)).astype(jnp.float32)
            attended = jnp.einsum("hij,jd->ihd", prob_half, value_window, precision=highest)
            row_delta = jnp.sum(grad_block * attended, axis=-1)
            value_part = jnp.einsum("hij,ihd->jd", prob_half, grad_block, precision=highest)
            grad_prob = jnp.einsum("ihd,jd->hij", grad_block, value_window, precision=highest)
            grad_score = attn_prob * (grad_prob - row_delta.T[:, :, None])
            grad_score = lax.optimization_barrier(grad_score.astype(jnp.bfloat16)).astype(jnp.float32)
            query_grad = jnp.einsum("hij,jd->ihd", grad_score, key_window, precision=highest) * score_scale
            key_part = jnp.einsum("hij,ihd->jd", grad_score, query_block, precision=highest) * score_scale
            key_accum = lax.dynamic_update_slice_in_dim(
                key_accum, lax.dynamic_slice_in_dim(key_accum, first, span, 0) + key_part, first, 0)
            value_accum = lax.dynamic_update_slice_in_dim(
                value_accum, lax.dynamic_slice_in_dim(value_accum, first, span, 0) + value_part, first, 0)
            return (key_accum, value_accum), (attended, query_grad)

        empty = jnp.zeros((TOKENS + width, HD), jnp.float32)
        sums, blocks = lax.scan(advance, (empty, empty), jnp.arange(N_CTX, dtype=jnp.int32))
        attended = blocks[0].reshape(TOKENS, GROUP, HD)
        query_grad = blocks[1].reshape(TOKENS, GROUP, HD)
        return attended, query_grad, sums[0][width:], sums[1][width:]

    attended, query_grad, key_grad, value_grad = lax.map(one_group, (query_heads, key_heads, value_heads, grad_heads))
    attended = attended.transpose(1, 0, 2, 3).reshape(TOKENS, HEADS * HD)
    query_grad = query_grad.transpose(1, 0, 2, 3).reshape(TOKENS, HEADS * HD)
    key_grad = key_grad.transpose(1, 0, 2).reshape(TOKENS, KV * HD)
    value_grad = value_grad.transpose(1, 0, 2).reshape(TOKENS, KV * HD)
    return (attended, query_grad, key_grad, value_grad)
```

```python
import math

import jax
import jax.numpy as jnp
from jax import lax
from jax.experimental import pallas as pl
from jax.experimental.pallas import tpu as pltpu
from jax.sharding import PartitionSpec as P

HD = 128
GROUP = 8
KV = 8
DEV = 128
HALF = 16
PIECE = (HALF, HD)
BLOCKS = 8
ROWS = 256
KEYS = 512
SPAN = ROWS // HALF
TOKENS_BLOCK = 512
SCALE = HD**-0.5
LOG2E = math.log2(math.e)
VERY_LOW = -1e30
NT = (((1,), (1,)), ((), ()))
MIB = 1 << 20


def mm(a, b):
    return jnp.dot(a, b, preferred_element_type=jnp.float32)


def mm_nt(a, b):
    return lax.dot_general(a, b, NT, preferred_element_type=jnp.float32)


def pack_kernel(q_ref, g_ref, k_ref, v_ref, out_ref):
    for hh in range(GROUP):
        for s in range(2):
            rows = slice(s * HALF, (s + 1) * HALF)
            for g in range(KV):
                to = (hh * 2 + s) * KV + g
                head = slice((g * GROUP + hh) * HD, (g * GROUP + hh + 1) * HD)
                group = slice(g * HD, (g + 1) * HD)
                out_ref[to, 0] = q_ref[rows, head]
                out_ref[to, 1] = g_ref[rows, head]
                out_ref[to, 2] = k_ref[rows, group]
                out_ref[to, 3] = v_ref[rows, group]


def attention_kernel(
    info_ref, got_ref, far_ref,
    odq_ref, own_ref, oth_ref,
    k_all, v_all, k_t, v_t, dk_acc, dv_acc, s_all, top, tot, o_t, dq_t,
):
    first_1, first_2, first_3, half = info_ref[0], info_ref[1], info_ref[2], info_ref[3]

    def doc_start(token):
        start = jnp.where(token >= first_1, first_1, 0)
        start = jnp.where(token >= first_2, first_2, start)
        return jnp.where(token >= first_3, first_3, start)

    def spread(r):
        return r + (r & ~(HALF - 1))

    def gather(j, carry):
        span = pl.ds(j * SPAN, SPAN)
        k_all[j, :ROWS] = got_ref[span, 2].reshape(ROWS, HD)
        k_all[j, ROWS:] = far_ref[span, 0].reshape(ROWS, HD)
        v_all[j, :ROWS] = got_ref[span, 3].reshape(ROWS, HD)
        v_all[j, ROWS:] = far_ref[span, 1].reshape(ROWS, HD)
        k_t[j] = k_all[j].T
        v_t[j] = v_all[j].T
        dk_acc[j] = jnp.zeros((KEYS, HD), jnp.float32)
        dv_acc[j] = jnp.zeros((KEYS, HD), jnp.float32)
        return carry

    lax.fori_loop(0, BLOCKS, gather, 0)

    def block(i, carry):
        span = pl.ds(i * SPAN, SPAN)
        q = got_ref[span, 0].reshape(ROWS, HD)
        g = got_ref[span, 1].reshape(ROWS, HD)
        first = i * TOKENS_BLOCK
        lo = doc_start(first) // TOKENS_BLOCK
        last_start = doc_start(first + TOKENS_BLOCK - 1)
        top[...] = jnp.full((8, ROWS), VERY_LOW, jnp.float32)

        def score(j, carry):
            def step(masked):
                s = mm_nt(k_all[j], q)
                if masked:
                    q_tok = first + HALF * half + spread(
                        lax.broadcasted_iota(jnp.int32, (1, ROWS), 1)
                    )
                    r = lax.broadcasted_iota(jnp.int32, (KEYS, ROWS), 0)
                    far = r >= ROWS
                    r = jnp.where(far, r - ROWS, r)
                    k_half = jnp.where(far, 1 - half, half)
                    k_tok = j * TOKENS_BLOCK + spread(r) + HALF * k_half
                    s = jnp.where((k_tok <= q_tok) & (k_tok >= doc_start(q_tok)), s, VERY_LOW)
                s_all[j] = s
                top[...] = jnp.maximum(top[...], jnp.max(s.reshape(KEYS // 8, 8, ROWS), axis=0))

            masked = (j == i) | (j * TOKENS_BLOCK < last_start)
            pl.when(masked)(lambda: step(True))
            pl.when(jnp.logical_not(masked))(lambda: step(False))
            return carry

        lax.fori_loop(lo, i + 1, score, 0)
        shift = jnp.max(top[...], axis=0, keepdims=True) * (SCALE * LOG2E)
        tot[...] = jnp.zeros((8, ROWS), jnp.float32)
        o_t[...] = jnp.zeros((HD, ROWS), jnp.float32)

        def mix(j, carry):
            e = jnp.exp2(s_all[j] * (SCALE * LOG2E) - shift)
            s_all[j] = e
            tot[...] += jnp.sum(e.reshape(KEYS // 8, 8, ROWS), axis=0)
            o_t[...] += mm(v_t[j], e.astype(jnp.bfloat16))
            return carry

        lax.fori_loop(lo, i + 1, mix, 0)
        inverse = 1.0 / jnp.sum(tot[...], axis=0, keepdims=True)
        o = (o_t[...] * inverse).T
        odq_ref[span, 0] = o.astype(jnp.bfloat16).reshape(SPAN, *PIECE)
        delta = jnp.sum((g.astype(jnp.float32) * o).T, axis=0, keepdims=True)
        dq_t[...] = jnp.zeros((HD, ROWS), jnp.float32)

        def back(j, carry):
            prob = s_all[j] * inverse
            d_prob = mm_nt(v_all[j], g)
            d_score = (prob * (d_prob - delta)).astype(jnp.bfloat16)
            dv_acc[j] += mm(prob.astype(jnp.bfloat16), g)
            dk_acc[j] += mm(d_score, q)
            dq_t[...] += mm(k_t[j], d_score)
            return carry

        lax.fori_loop(lo, i + 1, back, 0)
        odq_ref[span, 1] = (dq_t[...] * SCALE).T.astype(jnp.bfloat16).reshape(SPAN, *PIECE)
        return carry

    lax.fori_loop(0, BLOCKS, block, 0)

    def give(j, carry):
        span = pl.ds(j * SPAN, SPAN)
        own_ref[span, 0] = (dk_acc[j, :ROWS] * SCALE).reshape(SPAN, *PIECE)
        own_ref[span, 1] = dv_acc[j, :ROWS].reshape(SPAN, *PIECE)
        oth_ref[span, 0] = (dk_acc[j, ROWS:] * SCALE).astype(jnp.bfloat16).reshape(SPAN, *PIECE)
        oth_ref[span, 1] = dv_acc[j, ROWS:].astype(jnp.bfloat16).reshape(SPAN, *PIECE)
        return carry

    lax.fori_loop(0, BLOCKS, give, 0)


def unpack_kernel(got_ref, o_ref, dq_ref, dk_ref, dv_ref):
    for s in range(2):
        rows = slice(s * HALF, (s + 1) * HALF)
        for g in range(KV):
            group = slice(g * HD, (g + 1) * HD)
            dk = jnp.zeros(PIECE, jnp.float32)
            dv = jnp.zeros(PIECE, jnp.float32)
            for hh in range(GROUP):
                at = (hh * 2 + s) * KV + g
                head = slice((g * GROUP + hh) * HD, (g * GROUP + hh + 1) * HD)
                o_ref[rows, head] = got_ref[at, 0].astype(jnp.float32)
                dq_ref[rows, head] = got_ref[at, 1].astype(jnp.float32)
                dk += got_ref[at, 2].astype(jnp.float32)
                dv += got_ref[at, 3].astype(jnp.float32)
            dk_ref[rows, group] = dk
            dv_ref[rows, group] = dv


def everyone(x):
    return lax.all_to_all(x, ("ctx", "tp"), 0, 0, tiled=True)


def swap_cores(x):
    return lax.ppermute(x, "ctx", [(c, c ^ 1) for c in range(16)])


def per_device(queries, keys, values, out_grad, doc_ids):
    bf16, f32 = jnp.bfloat16, jnp.float32
    sent = pl.pallas_call(
        pack_kernel,
        out_shape=jax.ShapeDtypeStruct((DEV, 4, *PIECE), bf16),
        compiler_params=pltpu.CompilerParams(vmem_limit_bytes=32 * MIB),
    )(queries, out_grad, keys, values)
    got = everyone(sent)
    far = swap_cores(got[:, 2:])
    firsts = jnp.sum(doc_ids[None, :] < jnp.arange(1, 4, dtype=jnp.int32)[:, None], axis=1)
    half = lax.axis_index("ctx") % 2
    info = jnp.concatenate([firsts.astype(jnp.int32), half.astype(jnp.int32)[None]])
    pair = (DEV, 2, *PIECE)
    odq, own, oth = pl.pallas_call(
        attention_kernel,
        out_shape=(
            jax.ShapeDtypeStruct(pair, bf16),
            jax.ShapeDtypeStruct(pair, f32),
            jax.ShapeDtypeStruct(pair, bf16),
        ),
        in_specs=[
            pl.BlockSpec(memory_space=pltpu.SMEM),
            pl.BlockSpec(memory_space=pltpu.VMEM),
            pl.BlockSpec(memory_space=pltpu.VMEM),
        ],
        scratch_shapes=[
            pltpu.VMEM((BLOCKS, KEYS, HD), bf16),
            pltpu.VMEM((BLOCKS, KEYS, HD), bf16),
            pltpu.VMEM((BLOCKS, HD, KEYS), bf16),
            pltpu.VMEM((BLOCKS, HD, KEYS), bf16),
            pltpu.VMEM((BLOCKS, KEYS, HD), f32),
            pltpu.VMEM((BLOCKS, KEYS, HD), f32),
            pltpu.VMEM((BLOCKS, KEYS, ROWS), f32),
            pltpu.VMEM((8, ROWS), f32),
            pltpu.VMEM((8, ROWS), f32),
            pltpu.VMEM((HD, ROWS), f32),
            pltpu.VMEM((HD, ROWS), f32),
        ],
        compiler_params=pltpu.CompilerParams(vmem_limit_bytes=48 * MIB),
    )(info, got, far)
    dkv = (own + swap_cores(oth).astype(f32)).astype(bf16)
    back = everyone(jnp.concatenate([odq, dkv], axis=1))
    return pl.pallas_call(
        unpack_kernel,
        out_shape=(
            jax.ShapeDtypeStruct((2 * HALF, KV * GROUP * HD), f32),
            jax.ShapeDtypeStruct((2 * HALF, KV * GROUP * HD), f32),
            jax.ShapeDtypeStruct((2 * HALF, KV * HD), f32),
            jax.ShapeDtypeStruct((2 * HALF, KV * HD), f32),
        ),
        compiler_params=pltpu.CompilerParams(vmem_limit_bytes=32 * MIB),
    )(back)


def solution(mesh):
    rows = P(("ctx", "tp"), None)
    return jax.shard_map(
        per_device,
        mesh=mesh,
        in_specs=(rows, rows, rows, rows, P()),
        out_specs=(rows, rows, rows, rows),
        check_vma=False,
    )
```

```python
import math

import jax
import jax.numpy as jnp
from jax import lax
from jax.experimental import pallas as pl
from jax.experimental.pallas import tpu as pltpu
from jax.sharding import PartitionSpec as P

HD = 128
GROUP = 8
KV = 8
DEV = 128
HALF = 16
PIECE = (HALF, HD)
TOKENS = 4096
ROWS_ALL = TOKENS // 2
ROWS = 512
FAR = 512
TILE = 256
BLOCKS = ROWS_ALL // ROWS
CHUNKS = ROWS_ALL // FAR
KEYS = 2 * FAR
ROW_SPAN = ROWS // HALF
KEY_SPAN = FAR // HALF
SCALE = HD**-0.5
LOG2E = math.log2(math.e)
VERY_LOW = -1e30
NT = (((1,), (1,)), ((), ()))
MIB = 1 << 20


def mm(a, b):
    return jnp.dot(a, b, preferred_element_type=jnp.float32)


def mm_nt(a, b):
    return lax.dot_general(a, b, NT, preferred_element_type=jnp.float32)


def pack_kernel(q_hbm, g_hbm, k_hbm, v_hbm, out_hbm, q_ref, g_ref, k_ref, v_ref, out_ref, sems):
    arrays = ((q_hbm, q_ref), (g_hbm, g_ref), (k_hbm, k_ref), (v_hbm, v_ref))
    arrived, left = [], []
    for g in range(KV):
        for n, (src, dst) in enumerate(arrays):
            width = src.shape[1] // KV
            columns = pl.ds(g * width, width)
            arrived.append(
                pltpu.make_async_copy(src.at[:, columns], dst.at[:, columns], sems.at[g, n])
            )
            arrived[-1].start()
    for g in range(KV):
        for copy in arrived[4 * g : 4 * g + 4]:
            copy.wait()
        for hh in range(GROUP):
            for s in range(2):
                rows = slice(s * HALF, (s + 1) * HALF)
                head = slice((g * GROUP + hh) * HD, (g * GROUP + hh + 1) * HD)
                group = slice(g * HD, (g + 1) * HD)
                to = hh * 2 + s
                out_ref[to, g, 0] = q_ref[rows, head]
                out_ref[to, g, 1] = g_ref[rows, head]
                out_ref[to, g, 2] = k_ref[rows, group]
                out_ref[to, g, 3] = v_ref[rows, group]
        left.append(pltpu.make_async_copy(out_ref.at[:, g], out_hbm.at[:, g], sems.at[g, 4]))
        left[-1].start()
    for copy in left:
        copy.wait()


def split_kernel(got_ref, own_ref):
    own_ref[...] = got_ref[:, 2:]


def attention_kernel(
    info_ref, got_ref, far_ref,
    odq_ref, own_ref, oth_ref,
    k_all, v_all, k_t, v_t, dk_acc, dv_acc, s_all, top, tot, o_t, dq_t,
):
    first_1, first_2, first_3, half = info_ref[0], info_ref[1], info_ref[2], info_ref[3]

    def doc_start(token):
        start = jnp.where(token >= first_1, first_1, 0)
        start = jnp.where(token >= first_2, first_2, start)
        return jnp.where(token >= first_3, first_3, start)

    def spread(r):
        return r + (r & ~(HALF - 1))

    def gather(j, carry):
        span = pl.ds(j * KEY_SPAN, KEY_SPAN)
        k_all[j, :FAR] = got_ref[span, 2].reshape(FAR, HD)
        k_all[j, FAR:] = far_ref[span, 0].reshape(FAR, HD)
        v_all[j, :FAR] = got_ref[span, 3].reshape(FAR, HD)
        v_all[j, FAR:] = far_ref[span, 1].reshape(FAR, HD)
        k_t[j] = k_all[j].T
        v_t[j] = v_all[j].T
        return carry

    lax.fori_loop(0, CHUNKS, gather, 0)
    tiles = [(h * FAR + t, t, h) for h in range(2) for t in range(0, FAR, TILE)]

    def block(i, carry):
        span = pl.ds(i * ROW_SPAN, ROW_SPAN)
        q = got_ref[span, 0].reshape(ROWS, HD)
        g = got_ref[span, 1].reshape(ROWS, HD)
        g_t = g.T
        first = i * KEYS
        lo = doc_start(first) // KEYS
        last_start = doc_start(first + KEYS - 1)
        q_tok = first + HALF * half + spread(lax.broadcasted_iota(jnp.int32, (1, ROWS), 1))
        q_start = doc_start(q_tok)

        def k_token(j, t, h):
            r = lax.broadcasted_iota(jnp.int32, (TILE, 1), 0)
            return j * KEYS + spread(t + r) + HALF * (half if h == 0 else 1 - half)

        def put_top(s, r0, new):
            m = jnp.max(s.reshape(TILE // 8, 8, ROWS - r0), axis=0)
            top[:, r0:] = m if new else jnp.maximum(top[:, r0:], m)

        for at, t, h in tiles:
            k_tok = k_token(i, t, h)
            s = mm_nt(k_all[i, at : at + TILE], q[t:])
            s = jnp.where((k_tok <= q_tok[:, t:]) & (k_tok >= q_start[:, t:]), s, VERY_LOW)
            s_all[i, at : at + TILE, t:] = s
            put_top(s, t, at == 0)

        def score(j, carry):
            def step(masked):
                for at, t, h in tiles:
                    s = mm_nt(k_all[j, at : at + TILE], q)
                    if masked:
                        s = jnp.where(k_token(j, t, h) >= q_start, s, VERY_LOW)
                    s_all[j, at : at + TILE] = s
                    put_top(s, 0, False)

            masked = j * KEYS < last_start
            pl.when(masked)(lambda: step(True))
            pl.when(jnp.logical_not(masked))(lambda: step(False))
            return carry

        lax.fori_loop(lo, i, score, 0)
        shift = jnp.max(top[...], axis=0, keepdims=True) * (SCALE * LOG2E)

        def mix_tile(j, at, r0):
            e = jnp.exp2(s_all[j, at : at + TILE, r0:] * (SCALE * LOG2E) - shift[:, r0:])
            s_all[j, at : at + TILE, r0:] = e
            e_sum = jnp.sum(e.reshape(TILE // 8, 8, ROWS - r0), axis=0)
            return e_sum, mm(v_t[j, :, at : at + TILE], e.astype(jnp.bfloat16))

        for at, t, h in tiles:
            e_sum, mixed = mix_tile(i, at, t)
            tot[:, t:] = e_sum if at == 0 else tot[:, t:] + e_sum
            o_t[:, t:] = mixed if at == 0 else o_t[:, t:] + mixed

        def mix(j, carry):
            for at, t, h in tiles:
                e_sum, mixed = mix_tile(j, at, 0)
                tot[...] += e_sum
                o_t[...] += mixed
            return carry

        lax.fori_loop(lo, i, mix, 0)
        inverse = 1.0 / jnp.sum(tot[...], axis=0, keepdims=True)
        out_t = o_t[...] * inverse
        odq_ref[span, 0] = out_t.T.astype(jnp.bfloat16).reshape(ROW_SPAN, *PIECE)
        delta = jnp.sum(g_t.astype(jnp.float32) * out_t, axis=0, keepdims=True)

        def back_tile(j, at, r0):
            prob = s_all[j, at : at + TILE, r0:] * inverse[:, r0:]
            d_prob = mm_nt(v_all[j, at : at + TILE], g[r0:])
            d_score = (prob * (d_prob - delta[:, r0:])).astype(jnp.bfloat16)
            return (
                mm(prob.astype(jnp.bfloat16), g[r0:]),
                mm(d_score, q[r0:]),
                mm(k_t[j, :, at : at + TILE], d_score),
            )

        for at, t, h in tiles:
            dv, dk, dq = back_tile(i, at, t)
            dv_acc[i, at : at + TILE] = dv
            dk_acc[i, at : at + TILE] = dk
            dq_t[:, t:] = dq if at == 0 else dq_t[:, t:] + dq

        def back(j, carry):
            for at, t, h in tiles:
                dv, dk, dq = back_tile(j, at, 0)
                dv_acc[j, at : at + TILE] += dv
                dk_acc[j, at : at + TILE] += dk
                dq_t[...] += dq
            return carry

        lax.fori_loop(lo, i, back, 0)
        odq_ref[span, 1] = (dq_t[...] * SCALE).T.astype(jnp.bfloat16).reshape(ROW_SPAN, *PIECE)
        return carry

    lax.fori_loop(0, BLOCKS, block, 0)

    def give(j, carry):
        span = pl.ds(j * KEY_SPAN, KEY_SPAN)
        dk = dk_acc[j] * SCALE
        dv = dv_acc[j]
        own_ref[span, 0] = dk[:FAR].reshape(KEY_SPAN, *PIECE)
        own_ref[span, 1] = dv[:FAR].reshape(KEY_SPAN, *PIECE)
        oth_ref[span, 0] = dk[FAR:].astype(jnp.bfloat16).reshape(KEY_SPAN, *PIECE)
        oth_ref[span, 1] = dv[FAR:].astype(jnp.bfloat16).reshape(KEY_SPAN, *PIECE)
        return carry

    lax.fori_loop(0, CHUNKS, give, 0)


def join_kernel(odq_ref, own_ref, back_ref, out_ref):
    out_ref[:, :2] = odq_ref[...]
    out_ref[:, 2:] = (own_ref[...] + back_ref[...].astype(jnp.float32)).astype(jnp.bfloat16)


def unpack_kernel(got_ref, o_hbm, dq_hbm, dk_hbm, dv_hbm, o_ref, dq_ref, dk_ref, dv_ref, sems):
    copies = []

    def send(src, dst):
        copies.append(pltpu.make_async_copy(src, dst, sems.at[len(copies)]))
        copies[-1].start()

    for g in range(KV):
        group = slice(g * HD, (g + 1) * HD)
        for s in range(2):
            rows = slice(s * HALF, (s + 1) * HALF)
            dk = jnp.zeros(PIECE, jnp.float32)
            dv = jnp.zeros(PIECE, jnp.float32)
            for hh in range(GROUP):
                at = (hh * 2 + s) * KV + g
                head = slice((g * GROUP + hh) * HD, (g * GROUP + hh + 1) * HD)
                o_ref[rows, head] = got_ref[at, 0].astype(jnp.float32)
                dq_ref[rows, head] = got_ref[at, 1].astype(jnp.float32)
                dk += got_ref[at, 2].astype(jnp.float32)
                dv += got_ref[at, 3].astype(jnp.float32)
            dk_ref[rows, group] = dk
            dv_ref[rows, group] = dv
        heads = pl.ds(g * GROUP * HD, GROUP * HD)
        send(o_ref.at[:, heads], o_hbm.at[:, heads])
        send(dq_ref.at[:, heads], dq_hbm.at[:, heads])
    send(dk_ref, dk_hbm)
    send(dv_ref, dv_hbm)
    for copy in copies:
        copy.wait()


def everyone(x):
    return lax.all_to_all(x, ("ctx", "tp"), 0, 0, tiled=True)


def swap_cores(x):
    return lax.ppermute(x, "ctx", [(c, c ^ 1) for c in range(16)])


def per_device(queries, keys, values, out_grad, doc_ids):
    bf16, f32 = jnp.bfloat16, jnp.float32
    wide, narrow = (2 * HALF, KV * GROUP * HD), (2 * HALF, KV * HD)
    hbm = pl.BlockSpec(memory_space=pltpu.HBM)
    packed = (DEV // KV, KV, 4, *PIECE)
    sent = pl.pallas_call(
        pack_kernel,
        out_shape=jax.ShapeDtypeStruct(packed, bf16),
        in_specs=[hbm] * 4,
        out_specs=hbm,
        scratch_shapes=[
            pltpu.VMEM(wide, bf16),
            pltpu.VMEM(wide, bf16),
            pltpu.VMEM(narrow, bf16),
            pltpu.VMEM(narrow, bf16),
            pltpu.VMEM(packed, bf16),
            pltpu.SemaphoreType.DMA((KV, 5)),
        ],
        compiler_params=pltpu.CompilerParams(vmem_limit_bytes=60 * MIB),
    )(queries, out_grad, keys, values).reshape(DEV, 4, *PIECE)
    got = everyone(sent)
    pair = (DEV, 2, *PIECE)
    near = pl.pallas_call(
        split_kernel,
        out_shape=jax.ShapeDtypeStruct(pair, bf16),
        compiler_params=pltpu.CompilerParams(vmem_limit_bytes=16 * MIB),
    )(got)
    far = swap_cores(near)
    firsts = jnp.sum(doc_ids[None, :] < jnp.arange(1, 4, dtype=jnp.int32)[:, None], axis=1)
    half = lax.axis_index("ctx") % 2
    info = jnp.concatenate([firsts.astype(jnp.int32), half.astype(jnp.int32)[None]])
    odq, own, oth = pl.pallas_call(
        attention_kernel,
        out_shape=(
            jax.ShapeDtypeStruct(pair, bf16),
            jax.ShapeDtypeStruct(pair, f32),
            jax.ShapeDtypeStruct(pair, bf16),
        ),
        in_specs=[
            pl.BlockSpec(memory_space=pltpu.SMEM),
            pl.BlockSpec(memory_space=pltpu.VMEM),
            pl.BlockSpec(memory_space=pltpu.VMEM),
        ],
        scratch_shapes=[
            pltpu.VMEM((CHUNKS, KEYS, HD), bf16),
            pltpu.VMEM((CHUNKS, KEYS, HD), bf16),
            pltpu.VMEM((CHUNKS, HD, KEYS), bf16),
            pltpu.VMEM((CHUNKS, HD, KEYS), bf16),
            pltpu.VMEM((CHUNKS, KEYS, HD), f32),
            pltpu.VMEM((CHUNKS, KEYS, HD), f32),
            pltpu.VMEM((CHUNKS, KEYS, ROWS), f32),
            pltpu.VMEM((8, ROWS), f32),
            pltpu.VMEM((8, ROWS), f32),
            pltpu.VMEM((HD, ROWS), f32),
            pltpu.VMEM((HD, ROWS), f32),
        ],
        compiler_params=pltpu.CompilerParams(vmem_limit_bytes=32 * MIB),
    )(info, got, far)
    back = everyone(
        pl.pallas_call(
            join_kernel,
            out_shape=jax.ShapeDtypeStruct((DEV, 4, *PIECE), bf16),
            compiler_params=pltpu.CompilerParams(vmem_limit_bytes=16 * MIB),
        )(odq, own, swap_cores(oth))
    )
    return pl.pallas_call(
        unpack_kernel,
        out_shape=(
            jax.ShapeDtypeStruct(wide, f32),
            jax.ShapeDtypeStruct(wide, f32),
            jax.ShapeDtypeStruct(narrow, f32),
            jax.ShapeDtypeStruct(narrow, f32),
        ),
        out_specs=[hbm] * 4,
        scratch_shapes=[
            pltpu.VMEM(wide, f32),
            pltpu.VMEM(wide, f32),
            pltpu.VMEM(narrow, f32),
            pltpu.VMEM(narrow, f32),
            pltpu.SemaphoreType.DMA((2 * KV + 2,)),
        ],
        compiler_params=pltpu.CompilerParams(vmem_limit_bytes=16 * MIB),
    )(back)


def solution(mesh):
    rows = P(("ctx", "tp"), None)
    return jax.shard_map(
        per_device,
        mesh=mesh,
        in_specs=(rows, rows, rows, rows, P()),
        out_specs=(rows, rows, rows, rows),
        check_vma=False,
    )
```

```python
import math

import jax
import jax.numpy as jnp
from jax import lax
from jax.experimental import pallas as pl
from jax.experimental.pallas import tpu as pltpu
from jax.sharding import PartitionSpec as P

HD = 128
GROUP = 8
KV = 8
DEV = 128
HALF = 16
PIECE = (HALF, HD)
TOKENS = 4096
ROWS = 512
FAR = ROWS
TILE = 256
TILES = range(0, FAR, TILE)
KEYS = 2 * FAR
BLOCKS = TOKENS // KEYS
STEPS = BLOCKS * (BLOCKS + 1) // 2
SPAN = ROWS // HALF
SCALE = HD**-0.5
LOG2E = math.log2(math.e)
VERY_LOW = -1e30
NT = (((1,), (1,)), ((), ()))
MIB = 1 << 20


def mm(a, b):
    return jnp.dot(a, b, preferred_element_type=jnp.float32)


def mm_nt(a, b):
    return lax.dot_general(a, b, NT, preferred_element_type=jnp.float32)


def pack_kernel(q_hbm, g_hbm, k_hbm, v_hbm, out_hbm, q_ref, g_ref, k_ref, v_ref, out_ref, sems):
    arrays = ((q_hbm, q_ref), (g_hbm, g_ref), (k_hbm, k_ref), (v_hbm, v_ref))
    arrived, left = [], []
    for g in range(KV):
        for n, (src, dst) in enumerate(arrays):
            width = src.shape[1] // KV
            columns = pl.ds(g * width, width)
            arrived.append(
                pltpu.make_async_copy(src.at[:, columns], dst.at[:, columns], sems.at[g, n])
            )
            arrived[-1].start()
    for g in range(KV):
        for copy in arrived[4 * g : 4 * g + 4]:
            copy.wait()
        for hh in range(GROUP):
            for s in range(2):
                rows = slice(s * HALF, (s + 1) * HALF)
                head = slice((g * GROUP + hh) * HD, (g * GROUP + hh + 1) * HD)
                group = slice(g * HD, (g + 1) * HD)
                to = hh * 2 + s
                out_ref[to, g, 0] = q_ref[rows, head]
                out_ref[to, g, 1] = g_ref[rows, head]
                out_ref[to, g, 2] = k_ref[rows, group]
                out_ref[to, g, 3] = v_ref[rows, group]
        left.append(pltpu.make_async_copy(out_ref.at[:, g], out_hbm.at[:, g], sems.at[g, 4]))
        left[-1].start()
    for copy in left:
        copy.wait()


def split_kernel(got_ref, own_ref):
    own_ref[...] = got_ref[:, 2:]


def doc_start_in(info_ref):
    first_1, first_2, first_3 = info_ref[0], info_ref[1], info_ref[2]

    def doc_start(token):
        start = jnp.where(token >= first_1, first_1, 0)
        start = jnp.where(token >= first_2, first_2, start)
        return jnp.where(token >= first_3, first_3, start)

    return doc_start


def spread(r):
    return r + (r & ~(HALF - 1))


def step_of(i, j):
    return i * (i + 1) // 2 + j


def score_rows(i, key_half, info_ref, q, keys, put, top):
    doc_start = doc_start_in(info_ref)
    first = i * KEYS
    q_tok = first + HALF * info_ref[3] + spread(lax.broadcasted_iota(jnp.int32, (1, ROWS), 1))
    q_start = doc_start(q_tok)

    def k_token(j, t):
        r = lax.broadcasted_iota(jnp.int32, (TILE, 1), 0)
        return j * KEYS + spread(t + r) + HALF * key_half

    def put_top(s, r0):
        top[:, r0:] = jnp.maximum(
            top[:, r0:], jnp.max(s.reshape(TILE // 8, 8, ROWS - r0), axis=0)
        )

    for t in TILES:
        k_tok = k_token(i, t)
        s = mm_nt(keys(i, t), q[t:])
        s = jnp.where((k_tok <= q_tok[:, t:]) & (k_tok >= q_start[:, t:]), s, VERY_LOW)
        put(i, t, t, s)
        put_top(s, t)

    for j in range(i):
        for t in TILES:
            s = jnp.where(k_token(j, t) >= q_start, mm_nt(keys(j, t), q), VERY_LOW)
            put(j, t, 0, s)
            put_top(s, 0)


def keys_of(ref, which):
    def keys(j, t):
        return ref[pl.ds(j * SPAN + t // HALF, TILE // HALF), which].reshape(TILE, HD)

    return keys


def turn(ref, which, out_ref, j):
    out_ref[j] = ref[pl.ds(j * SPAN, SPAN), which].reshape(FAR, HD).T


def near_kernel(info_ref, got_ref, near_ref, s_near, top_near, k_t, v_t):
    def turns(j, carry):
        turn(near_ref, 0, k_t, j)
        turn(near_ref, 1, v_t, j)
        return carry

    lax.fori_loop(0, BLOCKS, turns, 0)

    def block(i, carry):
        q = got_ref[pl.ds(i * SPAN, SPAN), 0].reshape(ROWS, HD)
        top = top_near.at[i]
        top[...] = jnp.full((8, ROWS), VERY_LOW, jnp.float32)

        def put(j, t, r0, s):
            s_near[step_of(i, j), t : t + TILE, r0:] = s

        score_rows(i, info_ref[3], info_ref, q, keys_of(near_ref, 0), put, top)
        return carry

    for i in range(BLOCKS):
        block(i, 0)


def far_kernel(
    info_ref, got_ref, far_ref, s_near, top_near, v_t_near,
    o_ref, dq_part, stats, oth_ref,
    k_t, v_t, dk_acc, dv_acc, s_far, top, tot, o_t,
):
    def turns(j, carry):
        turn(far_ref, 0, k_t, j)
        turn(far_ref, 1, v_t, j)
        return carry

    lax.fori_loop(0, BLOCKS, turns, 0)
    k_far, v_far = keys_of(far_ref, 0), keys_of(far_ref, 1)

    def rows_of(i, which):
        return got_ref[i * SPAN : (i + 1) * SPAN, which].reshape(ROWS, HD)

    for i in range(BLOCKS):
        top[i] = top_near[i]

        def put(j, t, r0, s):
            s_far[step_of(i, j), t : t + TILE, r0:] = s

        score_rows(i, 1 - info_ref[3], info_ref, rows_of(i, 0), k_far, put, top.at[i])

    for i in range(BLOCKS):
        shift = jnp.max(top[i], axis=0, keepdims=True) * (SCALE * LOG2E)

        def mix_tile(j, t, r0):
            at = step_of(i, j)
            e_near = jnp.exp2(s_near[at, t : t + TILE, r0:] * (SCALE * LOG2E) - shift[:, r0:])
            e_far = jnp.exp2(s_far[at, t : t + TILE, r0:] * (SCALE * LOG2E) - shift[:, r0:])
            s_far[at, t : t + TILE, r0:] = e_far
            e_sum = jnp.sum((e_near + e_far).reshape(TILE // 8, 8, ROWS - r0), axis=0)
            mixed = mm(v_t_near[j, :, t : t + TILE], e_near.astype(jnp.bfloat16))
            return e_sum, mixed + mm(v_t[j, :, t : t + TILE], e_far.astype(jnp.bfloat16))

        for t in TILES:
            e_sum, mixed = mix_tile(i, t, t)
            tot[i, :, t:] = e_sum if t == 0 else tot[i, :, t:] + e_sum
            o_t[i, :, t:] = mixed if t == 0 else o_t[i, :, t:] + mixed
        for j in range(i):
            for t in TILES:
                e_sum, mixed = mix_tile(j, t, 0)
                tot[i] += e_sum
                o_t[i] += mixed

    for i in range(BLOCKS):
        span = slice(i * SPAN, (i + 1) * SPAN)
        shift = jnp.max(top[i], axis=0, keepdims=True) * (SCALE * LOG2E)
        total = jnp.sum(tot[i], axis=0, keepdims=True)
        inverse = 1.0 / total
        out_t = o_t[i] * inverse
        o_ref[span] = out_t.T.astype(jnp.bfloat16).reshape(SPAN, *PIECE)
        delta = jnp.sum(rows_of(i, 1).T.astype(jnp.float32) * out_t, axis=0, keepdims=True)
        stats[i, 0] = jnp.broadcast_to(shift + jnp.log(total) * LOG2E, (8, ROWS))
        stats[i, 1] = jnp.broadcast_to(delta, (8, ROWS))
        tot[i] = jnp.broadcast_to(inverse, (8, ROWS))

    for i in range(BLOCKS):
        q, g = rows_of(i, 0), rows_of(i, 1)
        inverse = tot[i, :1]
        delta = stats[i, 1, :1]

        def back_tile(j, t, r0):
            prob = s_far[step_of(i, j), t : t + TILE, r0:] * inverse[:, r0:]
            d_prob = mm_nt(v_far(j, t), g[r0:])
            d_score = (prob * (d_prob - delta[:, r0:])).astype(jnp.bfloat16)
            return (
                mm(prob.astype(jnp.bfloat16), g[r0:]),
                mm(d_score, q[r0:]),
                mm(k_t[j, :, t : t + TILE], d_score),
            )

        back_rows(i, back_tile, dv_acc, dk_acc, dq_part.at[i])

    def give(j, carry):
        span = pl.ds(j * SPAN, SPAN)
        oth_ref[span, 0] = (dk_acc[j] * SCALE).astype(jnp.bfloat16).reshape(SPAN, *PIECE)
        oth_ref[span, 1] = dv_acc[j].astype(jnp.bfloat16).reshape(SPAN, *PIECE)
        return carry

    lax.fori_loop(0, BLOCKS, give, 0)


def back_rows(i, back_tile, dv_acc, dk_acc, dq_t):
    for t in TILES:
        dv, dk, dq = back_tile(i, t, t)
        dv_acc[i, t : t + TILE] = dv
        dk_acc[i, t : t + TILE] = dk
        dq_t[:, t:] = dq if t == 0 else dq_t[:, t:] + dq

    for j in range(i):
        for t in TILES:
            dv, dk, dq = back_tile(j, t, 0)
            dv_acc[j, t : t + TILE] += dv
            dk_acc[j, t : t + TILE] += dk
            dq_t[...] += dq


def own_kernel(
    got_ref, near_ref, s_near, k_t, stats, dq_part,
    dq_ref, own_ref,
    dk_acc, dv_acc, dq_t,
):
    v_near = keys_of(near_ref, 1)

    def block(i, carry):
        span = pl.ds(i * SPAN, SPAN)
        q = got_ref[span, 0].reshape(ROWS, HD)
        g = got_ref[span, 1].reshape(ROWS, HD)
        log_total = stats[i, 0, :1]
        delta = stats[i, 1, :1]

        def back_tile(j, t, r0):
            s = s_near[step_of(i, j), t : t + TILE, r0:]
            prob = jnp.exp2(s * (SCALE * LOG2E) - log_total[:, r0:])
            d_prob = mm_nt(v_near(j, t), g[r0:])
            d_score = (prob * (d_prob - delta[:, r0:])).astype(jnp.bfloat16)
            return (
                mm(prob.astype(jnp.bfloat16), g[r0:]),
                mm(d_score, q[r0:]),
                mm(k_t[j, :, t : t + TILE], d_score),
            )

        back_rows(i, back_tile, dv_acc, dk_acc, dq_t)
        dq = (dq_t[...] + dq_part[i]) * SCALE
        dq_ref[span] = dq.T.astype(jnp.bfloat16).reshape(SPAN, *PIECE)
        return carry

    for i in range(BLOCKS):
        block(i, 0)

    def give(j, carry):
        span = pl.ds(j * SPAN, SPAN)
        own_ref[span, 0] = (dk_acc[j] * SCALE).reshape(SPAN, *PIECE)
        own_ref[span, 1] = dv_acc[j].reshape(SPAN, *PIECE)
        return carry

    lax.fori_loop(0, BLOCKS, give, 0)


def join_kernel(o_ref, dq_ref, own_ref, back_ref, out_ref):
    out_ref[:, 0] = o_ref[...]
    out_ref[:, 1] = dq_ref[...]
    out_ref[:, 2:] = (own_ref[...] + back_ref[...].astype(jnp.float32)).astype(jnp.bfloat16)


def unpack_kernel(got_ref, o_hbm, dq_hbm, dk_hbm, dv_hbm, o_ref, dq_ref, dk_ref, dv_ref, sems):
    copies = []

    def send(src, dst):
        copies.append(pltpu.make_async_copy(src, dst, sems.at[len(copies)]))
        copies[-1].start()

    for g in range(KV):
        group = slice(g * HD, (g + 1) * HD)
        for s in range(2):
            rows = slice(s * HALF, (s + 1) * HALF)
            dk = jnp.zeros(PIECE, jnp.float32)
            dv = jnp.zeros(PIECE, jnp.float32)
            for hh in range(GROUP):
                at = (hh * 2 + s) * KV + g
                head = slice((g * GROUP + hh) * HD, (g * GROUP + hh + 1) * HD)
                o_ref[rows, head] = got_ref[at, 0].astype(jnp.float32)
                dq_ref[rows, head] = got_ref[at, 1].astype(jnp.float32)
                dk += got_ref[at, 2].astype(jnp.float32)
                dv += got_ref[at, 3].astype(jnp.float32)
            dk_ref[rows, group] = dk
            dv_ref[rows, group] = dv
        heads = pl.ds(g * GROUP * HD, GROUP * HD)
        send(o_ref.at[:, heads], o_hbm.at[:, heads])
        send(dq_ref.at[:, heads], dq_hbm.at[:, heads])
    send(dk_ref, dk_hbm)
    send(dv_ref, dv_hbm)
    for copy in copies:
        copy.wait()


def everyone(x):
    return lax.all_to_all(x, ("ctx", "tp"), 0, 0, tiled=True)


def swap_cores(x):
    return lax.ppermute(x, "ctx", [(c, c ^ 1) for c in range(16)])


def per_device(queries, keys, values, out_grad, doc_ids):
    bf16, f32 = jnp.bfloat16, jnp.float32
    wide, narrow = (2 * HALF, KV * GROUP * HD), (2 * HALF, KV * HD)
    hbm = pl.BlockSpec(memory_space=pltpu.HBM)
    packed = (DEV // KV, KV, 4, *PIECE)
    sent = pl.pallas_call(
        pack_kernel,
        out_shape=jax.ShapeDtypeStruct(packed, bf16),
        in_specs=[hbm] * 4,
        out_specs=hbm,
        scratch_shapes=[
            pltpu.VMEM(wide, bf16),
            pltpu.VMEM(wide, bf16),
            pltpu.VMEM(narrow, bf16),
            pltpu.VMEM(narrow, bf16),
            pltpu.VMEM(packed, bf16),
            pltpu.SemaphoreType.DMA((KV, 5)),
        ],
        compiler_params=pltpu.CompilerParams(vmem_limit_bytes=60 * MIB),
    )(queries, out_grad, keys, values).reshape(DEV, 4, *PIECE)
    got = everyone(sent)
    pair = (DEV, 2, *PIECE)
    near = pl.pallas_call(
        split_kernel,
        out_shape=jax.ShapeDtypeStruct(pair, bf16),
        compiler_params=pltpu.CompilerParams(vmem_limit_bytes=16 * MIB),
    )(got)
    far = swap_cores(near)
    firsts = jnp.sum(doc_ids[None, :] < jnp.arange(1, 4, dtype=jnp.int32)[:, None], axis=1)
    half = lax.axis_index("ctx") % 2
    info = jnp.concatenate([firsts.astype(jnp.int32), half.astype(jnp.int32)[None]])
    smem = pl.BlockSpec(memory_space=pltpu.SMEM)
    vmem = pl.BlockSpec(memory_space=pltpu.VMEM)

    def out(shape, dtype):
        return jax.ShapeDtypeStruct(shape, dtype)

    def cost(flops):
        return pl.CostEstimate(flops=int(flops), bytes_accessed=MIB, transcendentals=0)

    single = (DEV, *PIECE)
    turned = (BLOCKS, HD, FAR)
    s_near, top_near, k_t, v_t = pl.pallas_call(
        near_kernel,
        out_shape=(
            out((STEPS, FAR, ROWS), f32),
            out((BLOCKS, 8, ROWS), f32),
            out(turned, bf16),
            out(turned, bf16),
        ),
        in_specs=[smem, vmem, vmem],
        compiler_params=pltpu.CompilerParams(vmem_limit_bytes=24 * MIB),
        cost_estimate=cost(4e9),
    )(info, got, near)
    o, dq_part, stats, oth = pl.pallas_call(
        far_kernel,
        out_shape=(
            out(single, bf16),
            out((BLOCKS, HD, ROWS), f32),
            out((BLOCKS, 2, 8, ROWS), f32),
            out(pair, bf16),
        ),
        in_specs=[smem] + [vmem] * 5,
        scratch_shapes=[
            pltpu.VMEM(turned, bf16),
            pltpu.VMEM(turned, bf16),
            pltpu.VMEM((BLOCKS, FAR, HD), f32),
            pltpu.VMEM((BLOCKS, FAR, HD), f32),
            pltpu.VMEM((STEPS, FAR, ROWS), f32),
            pltpu.VMEM((BLOCKS, 8, ROWS), f32),
            pltpu.VMEM((BLOCKS, 8, ROWS), f32),
            pltpu.VMEM((BLOCKS, HD, ROWS), f32),
        ],
        compiler_params=pltpu.CompilerParams(vmem_limit_bytes=32 * MIB),
        cost_estimate=cost(16e9),
    )(info, got, far, s_near, top_near, v_t)
    back = swap_cores(oth)
    dq, own = pl.pallas_call(
        own_kernel,
        out_shape=(out(single, bf16), out(pair, f32)),
        in_specs=[vmem] * 6,
        scratch_shapes=[
            pltpu.VMEM((BLOCKS, FAR, HD), f32),
            pltpu.VMEM((BLOCKS, FAR, HD), f32),
            pltpu.VMEM((HD, ROWS), f32),
        ],
        compiler_params=pltpu.CompilerParams(vmem_limit_bytes=28 * MIB),
        cost_estimate=cost(8e9),
    )(got, near, s_near, k_t, stats, dq_part)
    returned = everyone(
        pl.pallas_call(
            join_kernel,
            out_shape=out((DEV, 4, *PIECE), bf16),
            compiler_params=pltpu.CompilerParams(vmem_limit_bytes=16 * MIB),
        )(o, dq, own, back)
    )
    return pl.pallas_call(
        unpack_kernel,
        out_shape=(
            jax.ShapeDtypeStruct(wide, f32),
            jax.ShapeDtypeStruct(wide, f32),
            jax.ShapeDtypeStruct(narrow, f32),
            jax.ShapeDtypeStruct(narrow, f32),
        ),
        out_specs=[hbm] * 4,
        scratch_shapes=[
            pltpu.VMEM(wide, f32),
            pltpu.VMEM(wide, f32),
            pltpu.VMEM(narrow, f32),
            pltpu.VMEM(narrow, f32),
            pltpu.SemaphoreType.DMA((2 * KV + 2,)),
        ],
        compiler_params=pltpu.CompilerParams(vmem_limit_bytes=16 * MIB),
    )(returned)


def solution(mesh):
    rows = P(("ctx", "tp"), None)
    return jax.shard_map(
        per_device,
        mesh=mesh,
        in_specs=(rows, rows, rows, rows, P()),
        out_specs=(rows, rows, rows, rows),
        check_vma=False,
    )
```

```python
import functools
import math

import jax
import jax.numpy as jnp
from jax import lax
from jax.experimental import pallas as pl
from jax.experimental.pallas import tpu as pltpu
from jax.sharding import PartitionSpec as P

HD = 128
GROUP = 8
KV = 8
DEV = 128
OWN = 16
PIECE = (OWN, HD)
TOKENS = 4096
ROWS = 512
FAR = ROWS
TILE = 256
TILES = range(0, FAR, TILE)
KEYS = 2 * FAR
BLOCKS = TOKENS // KEYS
STEPS = BLOCKS * (BLOCKS + 1) // 2
SPAN = ROWS // OWN
SCALE = HD**-0.5
LOG2E = math.log2(math.e)
VERY_LOW = -1e30
NT = (((1,), (1,)), ((), ()))
MIB = 1 << 20


def mm(a, b):
    return jnp.dot(a, b, preferred_element_type=jnp.float32)


def mm_nt(a, b):
    return lax.dot_general(a, b, NT, preferred_element_type=jnp.float32)


def pack_kernel(q_hbm, g_hbm, k_hbm, v_hbm, out_hbm, q_ref, g_ref, k_ref, v_ref, out_ref, sems):
    arrays = ((q_hbm, q_ref), (g_hbm, g_ref), (k_hbm, k_ref), (v_hbm, v_ref))
    arrived, left = [], []
    for g in range(KV):
        for n, (src, dst) in enumerate(arrays):
            width = src.shape[1] // KV
            columns = pl.ds(g * width, width)
            arrived.append(
                pltpu.make_async_copy(src.at[:, columns], dst.at[:, columns], sems.at[g, n])
            )
            arrived[-1].start()
    for g in range(KV):
        for copy in arrived[4 * g : 4 * g + 4]:
            copy.wait()
        for hh in range(GROUP):
            for s in range(2):
                rows = slice(s * OWN, (s + 1) * OWN)
                head = slice((g * GROUP + hh) * HD, (g * GROUP + hh + 1) * HD)
                group = slice(g * HD, (g + 1) * HD)
                to = hh * 2 + s
                out_ref[to, g, 0] = q_ref[rows, head]
                out_ref[to, g, 1] = g_ref[rows, head]
                out_ref[to, g, 2] = k_ref[rows, group]
                out_ref[to, g, 3] = v_ref[rows, group]
        left.append(pltpu.make_async_copy(out_ref.at[:, g], out_hbm.at[:, g], sems.at[g, 4]))
        left[-1].start()
    for copy in left:
        copy.wait()


def split_kernel(got_ref, own_ref):
    own_ref[...] = got_ref[:, 2:]


def doc_start_in(info_ref):
    first_1, first_2, first_3 = info_ref[0], info_ref[1], info_ref[2]

    def doc_start(token):
        start = jnp.where(token >= first_1, first_1, 0)
        start = jnp.where(token >= first_2, first_2, start)
        return jnp.where(token >= first_3, first_3, start)

    return doc_start


def spread(r):
    return r + (r & ~(OWN - 1))


def step_of(i, j):
    return i * (i + 1) // 2 + j


def score_tiles(i, key_half, info_ref, q, keys, put, top):
    doc_start = doc_start_in(info_ref)
    first = i * KEYS
    q_tok = first + OWN * info_ref[3] + spread(lax.broadcasted_iota(jnp.int32, (1, ROWS), 1))
    q_start = doc_start(q_tok)

    def k_token(j, t):
        r = lax.broadcasted_iota(jnp.int32, (TILE, 1), 0)
        return j * KEYS + spread(t + r) + OWN * key_half

    def put_top(s, r0):
        top[:, r0:] = jnp.maximum(
            top[:, r0:], jnp.max(s.reshape(TILE // 8, 8, ROWS - r0), axis=0)
        )

    def diagonal(t):
        k_tok = k_token(i, t)
        s = mm_nt(keys(i, t), q[t:])
        s = jnp.where((k_tok <= q_tok[:, t:]) & (k_tok >= q_start[:, t:]), s, VERY_LOW)
        put(i, t, t, s)
        put_top(s, t)

    def full(j, t):
        s = jnp.where(k_token(j, t) >= q_start, mm_nt(keys(j, t), q), VERY_LOW)
        put(j, t, 0, s)
        put_top(s, 0)

    return [functools.partial(diagonal, t) for t in TILES] + [
        functools.partial(full, j, t) for j in range(i) for t in TILES
    ]


def run(steps):
    for step in steps:
        step()


def beside(one, other):
    placed = [((n + 0.5) / len(steps), k, step) for k, steps in enumerate((one, other))
              for n, step in enumerate(steps)]
    return [step for _, _, step in sorted(placed, key=lambda item: item[:2])]


def keys_of(ref, which):
    def keys(j, t):
        return ref[pl.ds(j * SPAN + t // OWN, TILE // OWN), which].reshape(TILE, HD)

    return keys


def turn(ref, which, out_ref, j):
    out_ref[j] = ref[pl.ds(j * SPAN, SPAN), which].reshape(FAR, HD).T


def near_kernel(info_ref, got_ref, near_ref, s_near, top_near, k_t, v_t):
    def turns(j, carry):
        turn(near_ref, 0, k_t, j)
        turn(near_ref, 1, v_t, j)
        return carry

    lax.fori_loop(0, BLOCKS, turns, 0)

    def block(i, carry):
        q = got_ref[pl.ds(i * SPAN, SPAN), 0].reshape(ROWS, HD)
        top = top_near.at[i]
        top[...] = jnp.full((8, ROWS), VERY_LOW, jnp.float32)

        def put(j, t, r0, s):
            s_near[step_of(i, j), t : t + TILE, r0:] = s

        run(score_tiles(i, info_ref[3], info_ref, q, keys_of(near_ref, 0), put, top))
        return carry

    for i in range(BLOCKS):
        block(i, 0)


def far_kernel(
    info_ref, got_ref, far_hbm, s_near, top_near, v_t_near,
    o_ref, dq_part, stats, oth_ref,
    far_ref, k_t, v_t, dk_acc, dv_acc, s_far, top, tot, o_t, sems,
):
    arriving = []
    for j in range(BLOCKS):
        span = pl.ds(j * SPAN, SPAN)
        arriving.append(pltpu.make_async_copy(far_hbm.at[span], far_ref.at[span], sems.at[j]))
        arriving[-1].start()
    k_far, v_far = keys_of(far_ref, 0), keys_of(far_ref, 1)

    def rows_of(i, which):
        return got_ref[i * SPAN : (i + 1) * SPAN, which].reshape(ROWS, HD)

    def scores(i):
        def put(j, t, r0, s):
            s_far[step_of(i, j), t : t + TILE, r0:] = s

        def begin():
            arriving[i].wait()
            top[i] = top_near[i]

        def end():
            turn(far_ref, 0, k_t, i)
            turn(far_ref, 1, v_t, i)

        tiles = score_tiles(i, 1 - info_ref[3], info_ref, rows_of(i, 0), k_far, put, top.at[i])
        return [begin, *tiles, end]

    def mixes(i):
        def shift():
            return jnp.max(top[i], axis=0, keepdims=True) * (SCALE * LOG2E)

        def tile(j, t, r0):
            at = step_of(i, j)
            e_near = jnp.exp2(s_near[at, t : t + TILE, r0:] * (SCALE * LOG2E) - shift()[:, r0:])
            e_far = jnp.exp2(s_far[at, t : t + TILE, r0:] * (SCALE * LOG2E) - shift()[:, r0:])
            s_far[at, t : t + TILE, r0:] = e_far
            e_sum = jnp.sum((e_near + e_far).reshape(TILE // 8, 8, ROWS - r0), axis=0)
            mixed = mm(v_t_near[j, :, t : t + TILE], e_near.astype(jnp.bfloat16))
            mixed += mm(v_t[j, :, t : t + TILE], e_far.astype(jnp.bfloat16))
            new = j == i and t == 0
            tot[i, :, r0:] = e_sum if new else tot[i, :, r0:] + e_sum
            o_t[i, :, r0:] = mixed if new else o_t[i, :, r0:] + mixed

        def end():
            span = slice(i * SPAN, (i + 1) * SPAN)
            total = jnp.sum(tot[i], axis=0, keepdims=True)
            inverse = 1.0 / total
            out_t = o_t[i] * inverse
            o_ref[span] = out_t.T.astype(jnp.bfloat16).reshape(SPAN, *PIECE)
            delta = jnp.sum(rows_of(i, 1).T.astype(jnp.float32) * out_t, axis=0, keepdims=True)
            stats[i, 0] = jnp.broadcast_to(shift() + jnp.log(total) * LOG2E, (8, ROWS))
            stats[i, 1] = jnp.broadcast_to(delta, (8, ROWS))
            tot[i] = jnp.broadcast_to(inverse, (8, ROWS))

        return [
            *(functools.partial(tile, i, t, t) for t in TILES),
            *(functools.partial(tile, j, t, 0) for j in range(i) for t in TILES),
            end,
        ]

    def backs(i):
        def tile(j, t, r0):
            q, g = rows_of(i, 0), rows_of(i, 1)
            prob = s_far[step_of(i, j), t : t + TILE, r0:] * tot[i, :1, r0:]
            d_prob = mm_nt(v_far(j, t), g[r0:])
            d_score = (prob * (d_prob - stats[i, 1, :1, r0:])).astype(jnp.bfloat16)
            return (
                mm(prob.astype(jnp.bfloat16), g[r0:]),
                mm(d_score, q[r0:]),
                mm(k_t[j, :, t : t + TILE], d_score),
            )

        return back_tiles(i, tile, dv_acc, dk_acc, dq_part.at[i])

    run(scores(0) + scores(1))
    run(beside(mixes(0) + mixes(1), scores(2)))
    run(beside(mixes(2), scores(3)))
    run(beside(mixes(3), backs(0) + backs(1) + backs(2)))
    run(backs(3))

    def give(j, carry):
        span = pl.ds(j * SPAN, SPAN)
        oth_ref[span, 0] = (dk_acc[j] * SCALE).astype(jnp.bfloat16).reshape(SPAN, *PIECE)
        oth_ref[span, 1] = dv_acc[j].astype(jnp.bfloat16).reshape(SPAN, *PIECE)
        return carry

    lax.fori_loop(0, BLOCKS, give, 0)


def back_tiles(i, back_tile, dv_acc, dk_acc, dq_t):
    def diagonal(t):
        dv, dk, dq = back_tile(i, t, t)
        dv_acc[i, t : t + TILE] = dv
        dk_acc[i, t : t + TILE] = dk
        dq_t[:, t:] = dq if t == 0 else dq_t[:, t:] + dq

    def full(j, t):
        dv, dk, dq = back_tile(j, t, 0)
        dv_acc[j, t : t + TILE] += dv
        dk_acc[j, t : t + TILE] += dk
        dq_t[...] += dq

    return [functools.partial(diagonal, t) for t in TILES] + [
        functools.partial(full, j, t) for j in range(i) for t in TILES
    ]


def own_kernel(
    got_ref, near_ref, s_near, k_t, stats, dq_part,
    dq_ref, own_ref,
    dk_acc, dv_acc, dq_t,
):
    v_near = keys_of(near_ref, 1)

    def block(i, carry):
        span = pl.ds(i * SPAN, SPAN)
        q = got_ref[span, 0].reshape(ROWS, HD)
        g = got_ref[span, 1].reshape(ROWS, HD)
        log_total = stats[i, 0, :1]
        delta = stats[i, 1, :1]

        def back_tile(j, t, r0):
            s = s_near[step_of(i, j), t : t + TILE, r0:]
            prob = jnp.exp2(s * (SCALE * LOG2E) - log_total[:, r0:])
            d_prob = mm_nt(v_near(j, t), g[r0:])
            d_score = (prob * (d_prob - delta[:, r0:])).astype(jnp.bfloat16)
            return (
                mm(prob.astype(jnp.bfloat16), g[r0:]),
                mm(d_score, q[r0:]),
                mm(k_t[j, :, t : t + TILE], d_score),
            )

        run(back_tiles(i, back_tile, dv_acc, dk_acc, dq_t))
        dq = (dq_t[...] + dq_part[i]) * SCALE
        dq_ref[span] = dq.T.astype(jnp.bfloat16).reshape(SPAN, *PIECE)
        return carry

    for i in range(BLOCKS):
        block(i, 0)

    def give(j, carry):
        span = pl.ds(j * SPAN, SPAN)
        own_ref[span, 0] = (dk_acc[j] * SCALE).reshape(SPAN, *PIECE)
        own_ref[span, 1] = dv_acc[j].reshape(SPAN, *PIECE)
        return carry

    lax.fori_loop(0, BLOCKS, give, 0)


def join_kernel(o_ref, dq_ref, own_ref, back_ref, out_ref):
    out_ref[:, 0] = o_ref[...]
    out_ref[:, 1] = dq_ref[...]
    out_ref[:, 2:] = (own_ref[...] + back_ref[...].astype(jnp.float32)).astype(jnp.bfloat16)


def unpack_kernel(got_ref, o_hbm, dq_hbm, dk_hbm, dv_hbm, o_ref, dq_ref, dk_ref, dv_ref, sems):
    copies = []

    def send(src, dst):
        copies.append(pltpu.make_async_copy(src, dst, sems.at[len(copies)]))
        copies[-1].start()

    for g in range(KV):
        group = slice(g * HD, (g + 1) * HD)
        for s in range(2):
            rows = slice(s * OWN, (s + 1) * OWN)
            dk = jnp.zeros(PIECE, jnp.float32)
            dv = jnp.zeros(PIECE, jnp.float32)
            for hh in range(GROUP):
                at = (hh * 2 + s) * KV + g
                head = slice((g * GROUP + hh) * HD, (g * GROUP + hh + 1) * HD)
                o_ref[rows, head] = got_ref[at, 0].astype(jnp.float32)
                dq_ref[rows, head] = got_ref[at, 1].astype(jnp.float32)
                dk += got_ref[at, 2].astype(jnp.float32)
                dv += got_ref[at, 3].astype(jnp.float32)
            dk_ref[rows, group] = dk
            dv_ref[rows, group] = dv
        heads = pl.ds(g * GROUP * HD, GROUP * HD)
        send(o_ref.at[:, heads], o_hbm.at[:, heads])
        send(dq_ref.at[:, heads], dq_hbm.at[:, heads])
    send(dk_ref, dk_hbm)
    send(dv_ref, dv_hbm)
    for copy in copies:
        copy.wait()


def everyone(x):
    return lax.all_to_all(x, ("ctx", "tp"), 0, 0, tiled=True)


def swap_cores(x):
    return lax.ppermute(x, "ctx", [(c, c ^ 1) for c in range(16)])


def per_device(queries, keys, values, out_grad, doc_ids):
    bf16, f32 = jnp.bfloat16, jnp.float32
    wide, narrow = (2 * OWN, KV * GROUP * HD), (2 * OWN, KV * HD)
    hbm = pl.BlockSpec(memory_space=pltpu.HBM)
    packed = (DEV // KV, KV, 4, *PIECE)
    sent = pl.pallas_call(
        pack_kernel,
        out_shape=jax.ShapeDtypeStruct(packed, bf16),
        in_specs=[hbm] * 4,
        out_specs=hbm,
        scratch_shapes=[
            pltpu.VMEM(wide, bf16),
            pltpu.VMEM(wide, bf16),
            pltpu.VMEM(narrow, bf16),
            pltpu.VMEM(narrow, bf16),
            pltpu.VMEM(packed, bf16),
            pltpu.SemaphoreType.DMA((KV, 5)),
        ],
        compiler_params=pltpu.CompilerParams(vmem_limit_bytes=60 * MIB),
    )(queries, out_grad, keys, values).reshape(DEV, 4, *PIECE)
    got = everyone(sent)
    pair = (DEV, 2, *PIECE)
    near = pl.pallas_call(
        split_kernel,
        out_shape=jax.ShapeDtypeStruct(pair, bf16),
        compiler_params=pltpu.CompilerParams(vmem_limit_bytes=16 * MIB),
    )(got)
    far = swap_cores(near)
    firsts = jnp.sum(doc_ids[None, :] < jnp.arange(1, 4, dtype=jnp.int32)[:, None], axis=1)
    half = lax.axis_index("ctx") % 2
    info = jnp.concatenate([firsts.astype(jnp.int32), half.astype(jnp.int32)[None]])
    smem = pl.BlockSpec(memory_space=pltpu.SMEM)
    vmem = pl.BlockSpec(memory_space=pltpu.VMEM)

    def out(shape, dtype):
        return jax.ShapeDtypeStruct(shape, dtype)

    def cost(flops):
        return pl.CostEstimate(flops=int(flops), bytes_accessed=MIB, transcendentals=0)

    single = (DEV, *PIECE)
    turned = (BLOCKS, HD, FAR)
    s_near, top_near, k_t, v_t = pl.pallas_call(
        near_kernel,
        out_shape=(
            out((STEPS, FAR, ROWS), f32),
            out((BLOCKS, 8, ROWS), f32),
            out(turned, bf16),
            out(turned, bf16),
        ),
        in_specs=[smem, vmem, vmem],
        compiler_params=pltpu.CompilerParams(vmem_limit_bytes=24 * MIB),
        cost_estimate=cost(4e9),
    )(info, got, near)
    o, dq_part, stats, oth = pl.pallas_call(
        far_kernel,
        out_shape=(
            out(single, bf16),
            out((BLOCKS, HD, ROWS), f32),
            out((BLOCKS, 2, 8, ROWS), f32),
            out(pair, bf16),
        ),
        in_specs=[smem, vmem, hbm] + [vmem] * 3,
        scratch_shapes=[
            pltpu.VMEM(pair, bf16),
            pltpu.VMEM(turned, bf16),
            pltpu.VMEM(turned, bf16),
            pltpu.VMEM((BLOCKS, FAR, HD), f32),
            pltpu.VMEM((BLOCKS, FAR, HD), f32),
            pltpu.VMEM((STEPS, FAR, ROWS), f32),
            pltpu.VMEM((BLOCKS, 8, ROWS), f32),
            pltpu.VMEM((BLOCKS, 8, ROWS), f32),
            pltpu.VMEM((BLOCKS, HD, ROWS), f32),
            pltpu.SemaphoreType.DMA((BLOCKS,)),
        ],
        compiler_params=pltpu.CompilerParams(vmem_limit_bytes=32 * MIB),
        cost_estimate=cost(16e9),
    )(info, got, far, s_near, top_near, v_t)
    back = swap_cores(oth)
    dq, own = pl.pallas_call(
        own_kernel,
        out_shape=(out(single, bf16), out(pair, f32)),
        in_specs=[vmem] * 6,
        scratch_shapes=[
            pltpu.VMEM((BLOCKS, FAR, HD), f32),
            pltpu.VMEM((BLOCKS, FAR, HD), f32),
            pltpu.VMEM((HD, ROWS), f32),
        ],
        compiler_params=pltpu.CompilerParams(vmem_limit_bytes=28 * MIB),
        cost_estimate=cost(8e9),
    )(got, near, s_near, k_t, stats, dq_part)
    returned = everyone(
        pl.pallas_call(
            join_kernel,
            out_shape=out((DEV, 4, *PIECE), bf16),
            compiler_params=pltpu.CompilerParams(vmem_limit_bytes=16 * MIB),
        )(o, dq, own, back)
    )
    return pl.pallas_call(
        unpack_kernel,
        out_shape=(
            jax.ShapeDtypeStruct(wide, f32),
            jax.ShapeDtypeStruct(wide, f32),
            jax.ShapeDtypeStruct(narrow, f32),
            jax.ShapeDtypeStruct(narrow, f32),
        ),
        out_specs=[hbm] * 4,
        scratch_shapes=[
            pltpu.VMEM(wide, f32),
            pltpu.VMEM(wide, f32),
            pltpu.VMEM(narrow, f32),
            pltpu.VMEM(narrow, f32),
            pltpu.SemaphoreType.DMA((2 * KV + 2,)),
        ],
        compiler_params=pltpu.CompilerParams(vmem_limit_bytes=16 * MIB),
    )(returned)


def solution(mesh):
    rows = P(("ctx", "tp"), None)
    return jax.shard_map(
        per_device,
        mesh=mesh,
        in_specs=(rows, rows, rows, rows, P()),
        out_specs=(rows, rows, rows, rows),
        check_vma=False,
    )
```

```python
import functools
import math

import jax
import jax.numpy as jnp
from jax import lax
from jax.experimental import pallas as pl
from jax.experimental.pallas import tpu as pltpu
from jax.sharding import PartitionSpec as P

HD = 128
GROUP = 8
KV = 8
DEV = 128
OWN = 16
PIECE = (OWN, HD)
TOKENS = 4096
ROWS = 512
FAR = ROWS
TILE = 256
TILES = range(0, FAR, TILE)
KEYS = 2 * FAR
BLOCKS = TOKENS // KEYS
STEPS = BLOCKS * (BLOCKS + 1) // 2
SPAN = ROWS // OWN
SCALE = HD**-0.5
LOG2E = math.log2(math.e)
VERY_LOW = -1e30
NT = (((1,), (1,)), ((), ()))
MIB = 1 << 20


def mm(a, b):
    return jnp.dot(a, b, preferred_element_type=jnp.float32)


def mm_nt(a, b):
    return lax.dot_general(a, b, NT, preferred_element_type=jnp.float32)


def pack_kernel(q_hbm, g_hbm, k_hbm, v_hbm, out_hbm, q_ref, g_ref, k_ref, v_ref, out_ref, sems):
    arrays = ((q_hbm, q_ref), (g_hbm, g_ref), (k_hbm, k_ref), (v_hbm, v_ref))
    arrived, left = [], []
    for g in range(KV):
        for n, (src, dst) in enumerate(arrays):
            width = src.shape[1] // KV
            columns = pl.ds(g * width, width)
            arrived.append(
                pltpu.make_async_copy(src.at[:, columns], dst.at[:, columns], sems.at[g, n])
            )
            arrived[-1].start()
    for g in range(KV):
        for copy in arrived[4 * g : 4 * g + 4]:
            copy.wait()
        for hh in range(GROUP):
            for s in range(2):
                rows = slice(s * OWN, (s + 1) * OWN)
                head = slice((g * GROUP + hh) * HD, (g * GROUP + hh + 1) * HD)
                group = slice(g * HD, (g + 1) * HD)
                to = hh * 2 + s
                out_ref[to, g, 0] = q_ref[rows, head]
                out_ref[to, g, 1] = g_ref[rows, head]
                out_ref[to, g, 2] = k_ref[rows, group]
                out_ref[to, g, 3] = v_ref[rows, group]
        left.append(pltpu.make_async_copy(out_ref.at[:, g], out_hbm.at[:, g], sems.at[g, 4]))
        left[-1].start()
    for copy in left:
        copy.wait()


def split_kernel(got_ref, own_ref):
    own_ref[...] = got_ref[:, 2:]


def doc_start_in(info_ref):
    first_1, first_2, first_3 = info_ref[0], info_ref[1], info_ref[2]

    def doc_start(token):
        start = jnp.where(token >= first_1, first_1, 0)
        start = jnp.where(token >= first_2, first_2, start)
        return jnp.where(token >= first_3, first_3, start)

    return doc_start


def spread(r):
    return r + (r & ~(OWN - 1))


def step_of(i, j):
    return i * (i + 1) // 2 + j


def score_tiles(i, key_half, info_ref, q, keys, put, top):
    doc_start = doc_start_in(info_ref)
    first = i * KEYS
    q_tok = first + OWN * info_ref[3] + spread(lax.broadcasted_iota(jnp.int32, (1, ROWS), 1))
    q_start = doc_start(q_tok)

    def k_token(j, t):
        r = lax.broadcasted_iota(jnp.int32, (TILE, 1), 0)
        return j * KEYS + spread(t + r) + OWN * key_half

    def put_top(s, r0):
        top[:, r0:] = jnp.maximum(
            top[:, r0:], jnp.max(s.reshape(TILE // 8, 8, ROWS - r0), axis=0)
        )

    def diagonal(t):
        k_tok = k_token(i, t)
        s = mm_nt(keys(i, t), q[t:])
        s = jnp.where((k_tok <= q_tok[:, t:]) & (k_tok >= q_start[:, t:]), s, VERY_LOW)
        put(i, t, t, s)
        put_top(s, t)

    def full(j, t):
        s = jnp.where(k_token(j, t) >= q_start, mm_nt(keys(j, t), q), VERY_LOW)
        put(j, t, 0, s)
        put_top(s, 0)

    return [functools.partial(diagonal, t) for t in TILES] + [
        functools.partial(full, j, t) for j in range(i) for t in TILES
    ]


def run(steps):
    for step in steps:
        step()


def beside(one, other):
    placed = [((n + 0.5) / len(steps), k, step) for k, steps in enumerate((one, other))
              for n, step in enumerate(steps)]
    return [step for _, _, step in sorted(placed, key=lambda item: item[:2])]


def keys_of(ref, which):
    def keys(j, t):
        return ref[pl.ds(j * SPAN + t // OWN, TILE // OWN), which].reshape(TILE, HD)

    return keys


def turn(ref, which, out_ref, j):
    out_ref[j] = ref[pl.ds(j * SPAN, SPAN), which].reshape(FAR, HD).T


def near_kernel(info_ref, got_ref, near_ref, s_near, top_near, k_t, v_t):
    def turns(j, carry):
        turn(near_ref, 0, k_t, j)
        turn(near_ref, 1, v_t, j)
        return carry

    lax.fori_loop(0, BLOCKS, turns, 0)

    def block(i, carry):
        q = got_ref[pl.ds(i * SPAN, SPAN), 0].reshape(ROWS, HD)
        top = top_near.at[i]
        top[...] = jnp.full((8, ROWS), VERY_LOW, jnp.float32)

        def put(j, t, r0, s):
            s_near[step_of(i, j), t : t + TILE, r0:] = s

        run(score_tiles(i, info_ref[3], info_ref, q, keys_of(near_ref, 0), put, top))
        return carry

    for i in range(BLOCKS):
        block(i, 0)


def far_kernel(
    info_ref, got_ref, far_hbm, s_near, top_near, v_t_near,
    o_ref, dq_part, stats, oth_ref,
    far_ref, k_t, v_t, dk_acc, dv_acc, s_far, top, tot, o_t, sems,
):
    arriving = []
    for j in range(BLOCKS):
        span = pl.ds(j * SPAN, SPAN)
        arriving.append(pltpu.make_async_copy(far_hbm.at[span], far_ref.at[span], sems.at[j]))
        arriving[-1].start()
    k_far, v_far = keys_of(far_ref, 0), keys_of(far_ref, 1)

    def rows_of(i, which):
        return got_ref[i * SPAN : (i + 1) * SPAN, which].reshape(ROWS, HD)

    def scores(i):
        def put(j, t, r0, s):
            s_far[step_of(i, j), t : t + TILE, r0:] = s

        def begin():
            arriving[i].wait()
            top[i] = top_near[i]

        def end():
            turn(far_ref, 0, k_t, i)
            turn(far_ref, 1, v_t, i)

        tiles = score_tiles(i, 1 - info_ref[3], info_ref, rows_of(i, 0), k_far, put, top.at[i])
        return [begin, *tiles, end]

    def mixes(i):
        def shift():
            return jnp.max(top[i], axis=0, keepdims=True) * (SCALE * LOG2E)

        def tile(j, t, r0):
            at = step_of(i, j)
            e_near = jnp.exp2(s_near[at, t : t + TILE, r0:] * (SCALE * LOG2E) - shift()[:, r0:])
            e_far = jnp.exp2(s_far[at, t : t + TILE, r0:] * (SCALE * LOG2E) - shift()[:, r0:])
            s_far[at, t : t + TILE, r0:] = e_far
            e_sum = jnp.sum((e_near + e_far).reshape(TILE // 8, 8, ROWS - r0), axis=0)
            mixed = mm(v_t_near[j, :, t : t + TILE], e_near.astype(jnp.bfloat16))
            mixed += mm(v_t[j, :, t : t + TILE], e_far.astype(jnp.bfloat16))
            new = j == i and t == 0
            tot[i, :, r0:] = e_sum if new else tot[i, :, r0:] + e_sum
            o_t[i, :, r0:] = mixed if new else o_t[i, :, r0:] + mixed

        def end():
            span = slice(i * SPAN, (i + 1) * SPAN)
            total = jnp.sum(tot[i], axis=0, keepdims=True)
            inverse = 1.0 / total
            out_t = o_t[i] * inverse
            o_ref[span] = out_t.T.astype(jnp.bfloat16).reshape(SPAN, *PIECE)
            delta = jnp.sum(rows_of(i, 1).T.astype(jnp.float32) * out_t, axis=0, keepdims=True)
            stats[i, 0] = jnp.broadcast_to(shift() + jnp.log(total) * LOG2E, (8, ROWS))
            stats[i, 1] = jnp.broadcast_to(delta, (8, ROWS))
            tot[i] = jnp.broadcast_to(inverse, (8, ROWS))

        return [
            *(functools.partial(tile, i, t, t) for t in TILES),
            *(functools.partial(tile, j, t, 0) for j in range(i) for t in TILES),
            end,
        ]

    def backs(i):
        def tile(j, t, r0):
            q, g = rows_of(i, 0), rows_of(i, 1)
            prob = s_far[step_of(i, j), t : t + TILE, r0:] * tot[i, :1, r0:]
            d_prob = mm_nt(v_far(j, t), g[r0:])
            d_score = (prob * (d_prob - stats[i, 1, :1, r0:])).astype(jnp.bfloat16)
            return (
                mm(prob.astype(jnp.bfloat16), g[r0:]),
                mm(d_score, q[r0:]),
                mm(k_t[j, :, t : t + TILE], d_score),
            )

        return back_tiles(i, tile, dv_acc, dk_acc, dq_part.at[i])

    run(scores(0) + scores(1))
    run(beside(mixes(0) + mixes(1), scores(2)))
    run(beside(mixes(2), scores(3) + backs(0)))
    run(beside(mixes(3), backs(1) + backs(2)))
    run(backs(3))

    def give(j, carry):
        span = pl.ds(j * SPAN, SPAN)
        oth_ref[span, 0] = (dk_acc[j] * SCALE).astype(jnp.bfloat16).reshape(SPAN, *PIECE)
        oth_ref[span, 1] = dv_acc[j].astype(jnp.bfloat16).reshape(SPAN, *PIECE)
        return carry

    lax.fori_loop(0, BLOCKS, give, 0)


def back_tiles(i, back_tile, dv_acc, dk_acc, dq_t):
    def diagonal(t):
        dv, dk, dq = back_tile(i, t, t)
        dv_acc[i, t : t + TILE] = dv
        dk_acc[i, t : t + TILE] = dk
        dq_t[:, t:] = dq if t == 0 else dq_t[:, t:] + dq

    def full(j, t):
        dv, dk, dq = back_tile(j, t, 0)
        dv_acc[j, t : t + TILE] += dv
        dk_acc[j, t : t + TILE] += dk
        dq_t[...] += dq

    return [functools.partial(diagonal, t) for t in TILES] + [
        functools.partial(full, j, t) for j in range(i) for t in TILES
    ]


def own_kernel(
    got_ref, near_ref, s_near, k_t, stats, dq_part,
    dq_ref, own_ref,
    dk_acc, dv_acc, dq_t,
):
    v_near = keys_of(near_ref, 1)

    def block(i, carry):
        span = pl.ds(i * SPAN, SPAN)
        q = got_ref[span, 0].reshape(ROWS, HD)
        g = got_ref[span, 1].reshape(ROWS, HD)
        log_total = stats[i, 0, :1]
        delta = stats[i, 1, :1]

        def back_tile(j, t, r0):
            s = s_near[step_of(i, j), t : t + TILE, r0:]
            prob = jnp.exp2(s * (SCALE * LOG2E) - log_total[:, r0:])
            d_prob = mm_nt(v_near(j, t), g[r0:])
            d_score = (prob * (d_prob - delta[:, r0:])).astype(jnp.bfloat16)
            return (
                mm(prob.astype(jnp.bfloat16), g[r0:]),
                mm(d_score, q[r0:]),
                mm(k_t[j, :, t : t + TILE], d_score),
            )

        run(back_tiles(i, back_tile, dv_acc, dk_acc, dq_t))
        dq = (dq_t[...] + dq_part[i]) * SCALE
        dq_ref[span] = dq.T.astype(jnp.bfloat16).reshape(SPAN, *PIECE)
        return carry

    for i in range(BLOCKS):
        block(i, 0)

    def give(j, carry):
        span = pl.ds(j * SPAN, SPAN)
        own_ref[span, 0] = (dk_acc[j] * SCALE).reshape(SPAN, *PIECE)
        own_ref[span, 1] = dv_acc[j].reshape(SPAN, *PIECE)
        return carry

    lax.fori_loop(0, BLOCKS, give, 0)


def join_kernel(o_ref, dq_ref, own_ref, back_ref, out_ref):
    out_ref[:, 0] = o_ref[...]
    out_ref[:, 1] = dq_ref[...]
    out_ref[:, 2:] = (own_ref[...] + back_ref[...].astype(jnp.float32)).astype(jnp.bfloat16)


def unpack_kernel(got_ref, o_hbm, dq_hbm, dk_hbm, dv_hbm, o_ref, dq_ref, dk_ref, dv_ref, sems):
    copies = []

    def send(src, dst):
        copies.append(pltpu.make_async_copy(src, dst, sems.at[len(copies)]))
        copies[-1].start()

    for g in range(KV):
        group = slice(g * HD, (g + 1) * HD)
        for s in range(2):
            rows = slice(s * OWN, (s + 1) * OWN)
            dk = jnp.zeros(PIECE, jnp.float32)
            dv = jnp.zeros(PIECE, jnp.float32)
            for hh in range(GROUP):
                at = (hh * 2 + s) * KV + g
                head = slice((g * GROUP + hh) * HD, (g * GROUP + hh + 1) * HD)
                o_ref[rows, head] = got_ref[at, 0].astype(jnp.float32)
                dq_ref[rows, head] = got_ref[at, 1].astype(jnp.float32)
                dk += got_ref[at, 2].astype(jnp.float32)
                dv += got_ref[at, 3].astype(jnp.float32)
            dk_ref[rows, group] = dk
            dv_ref[rows, group] = dv
        heads = pl.ds(g * GROUP * HD, GROUP * HD)
        send(o_ref.at[:, heads], o_hbm.at[:, heads])
        send(dq_ref.at[:, heads], dq_hbm.at[:, heads])
    send(dk_ref, dk_hbm)
    send(dv_ref, dv_hbm)
    for copy in copies:
        copy.wait()


def everyone(x):
    return lax.all_to_all(x, ("ctx", "tp"), 0, 0, tiled=True)


def swap_cores(x):
    return lax.ppermute(x, "ctx", [(c, c ^ 1) for c in range(16)])


def per_device(queries, keys, values, out_grad, doc_ids):
    bf16, f32 = jnp.bfloat16, jnp.float32
    wide, narrow = (2 * OWN, KV * GROUP * HD), (2 * OWN, KV * HD)
    hbm = pl.BlockSpec(memory_space=pltpu.HBM)
    packed = (DEV // KV, KV, 4, *PIECE)
    sent = pl.pallas_call(
        pack_kernel,
        out_shape=jax.ShapeDtypeStruct(packed, bf16),
        in_specs=[hbm] * 4,
        out_specs=hbm,
        scratch_shapes=[
            pltpu.VMEM(wide, bf16),
            pltpu.VMEM(wide, bf16),
            pltpu.VMEM(narrow, bf16),
            pltpu.VMEM(narrow, bf16),
            pltpu.VMEM(packed, bf16),
            pltpu.SemaphoreType.DMA((KV, 5)),
        ],
        compiler_params=pltpu.CompilerParams(vmem_limit_bytes=60 * MIB),
    )(queries, out_grad, keys, values).reshape(DEV, 4, *PIECE)
    got = everyone(sent)
    pair = (DEV, 2, *PIECE)
    near = pl.pallas_call(
        split_kernel,
        out_shape=jax.ShapeDtypeStruct(pair, bf16),
        compiler_params=pltpu.CompilerParams(vmem_limit_bytes=16 * MIB),
    )(got)
    far = swap_cores(near)
    firsts = jnp.sum(doc_ids[None, :] < jnp.arange(1, 4, dtype=jnp.int32)[:, None], axis=1)
    half = lax.axis_index("ctx") % 2
    info = jnp.concatenate([firsts.astype(jnp.int32), half.astype(jnp.int32)[None]])
    smem = pl.BlockSpec(memory_space=pltpu.SMEM)
    vmem = pl.BlockSpec(memory_space=pltpu.VMEM)

    def out(shape, dtype):
        return jax.ShapeDtypeStruct(shape, dtype)

    def cost(flops):
        return pl.CostEstimate(flops=int(flops), bytes_accessed=MIB, transcendentals=0)

    single = (DEV, *PIECE)
    turned = (BLOCKS, HD, FAR)
    s_near, top_near, k_t, v_t = pl.pallas_call(
        near_kernel,
        out_shape=(
            out((STEPS, FAR, ROWS), f32),
            out((BLOCKS, 8, ROWS), f32),
            out(turned, bf16),
            out(turned, bf16),
        ),
        in_specs=[smem, vmem, vmem],
        compiler_params=pltpu.CompilerParams(vmem_limit_bytes=24 * MIB),
        cost_estimate=cost(4e9),
    )(info, got, near)
    o, dq_part, stats, oth = pl.pallas_call(
        far_kernel,
        out_shape=(
            out(single, bf16),
            out((BLOCKS, HD, ROWS), f32),
            out((BLOCKS, 2, 8, ROWS), f32),
            out(pair, bf16),
        ),
        in_specs=[smem, vmem, hbm] + [vmem] * 3,
        scratch_shapes=[
            pltpu.VMEM(pair, bf16),
            pltpu.VMEM(turned, bf16),
            pltpu.VMEM(turned, bf16),
            pltpu.VMEM((BLOCKS, FAR, HD), f32),
            pltpu.VMEM((BLOCKS, FAR, HD), f32),
            pltpu.VMEM((STEPS, FAR, ROWS), f32),
            pltpu.VMEM((BLOCKS, 8, ROWS), f32),
            pltpu.VMEM((BLOCKS, 8, ROWS), f32),
            pltpu.VMEM((BLOCKS, HD, ROWS), f32),
            pltpu.SemaphoreType.DMA((BLOCKS,)),
        ],
        compiler_params=pltpu.CompilerParams(vmem_limit_bytes=32 * MIB),
        cost_estimate=cost(16e9),
    )(info, got, far, s_near, top_near, v_t)
    back = swap_cores(oth)
    dq, own = pl.pallas_call(
        own_kernel,
        out_shape=(out(single, bf16), out(pair, f32)),
        in_specs=[vmem] * 6,
        scratch_shapes=[
            pltpu.VMEM((BLOCKS, FAR, HD), f32),
            pltpu.VMEM((BLOCKS, FAR, HD), f32),
            pltpu.VMEM((HD, ROWS), f32),
        ],
        compiler_params=pltpu.CompilerParams(vmem_limit_bytes=28 * MIB),
        cost_estimate=cost(8e9),
    )(got, near, s_near, k_t, stats, dq_part)
    returned = everyone(
        pl.pallas_call(
            join_kernel,
            out_shape=out((DEV, 4, *PIECE), bf16),
            compiler_params=pltpu.CompilerParams(vmem_limit_bytes=16 * MIB),
        )(o, dq, own, back)
    )
    return pl.pallas_call(
        unpack_kernel,
        out_shape=(
            jax.ShapeDtypeStruct(wide, f32),
            jax.ShapeDtypeStruct(wide, f32),
            jax.ShapeDtypeStruct(narrow, f32),
            jax.ShapeDtypeStruct(narrow, f32),
        ),
        out_specs=[hbm] * 4,
        scratch_shapes=[
            pltpu.VMEM(wide, f32),
            pltpu.VMEM(wide, f32),
            pltpu.VMEM(narrow, f32),
            pltpu.VMEM(narrow, f32),
            pltpu.SemaphoreType.DMA((2 * KV + 2,)),
        ],
        compiler_params=pltpu.CompilerParams(vmem_limit_bytes=16 * MIB),
    )(returned)


def solution(mesh):
    rows = P(("ctx", "tp"), None)
    return jax.shard_map(
        per_device,
        mesh=mesh,
        in_specs=(rows, rows, rows, rows, P()),
        out_specs=(rows, rows, rows, rows),
        check_vma=False,
    )
```
